32 devices in a mesh: row: 2 (over x), col: 4 (over z), depth: 4 (over y, core).
Axes of the slice: x: 2, y: 2, z: 4, core: 2. Of those that a mesh axis runs over, the one named last changes fastest.
Arguments:
- trailing: float32 [8192, 8192], P('row', 'col'), may hold values from -6 to 6
- panel: bfloat16 [8192, 4096], P('row', 'col'), may hold values from -0.75 to 0.75
- inverse_factor: bfloat16 [4096, 4096], P('depth', 'col'), may hold values from -0.09375 to 0.09375
- block_inverse: float32 [8192, 512], P('row'), may hold values from -0.25 to 0.25
- guess: float32 [8192, 128], P(('col', 'depth')), may hold values from -0.0625 to 0.0625
- target: float32 [8192, 128], P('row'), may hold values from -6 to 6
Outputs:
- updated: float32 [8192, 8192], P('row', ('col', 'depth'))
- correction: float32 [8192, 128], P('row')
- residual_rms: float32 [1], replicated
The draws below stay inside these ranges and needn't reach their ends.
All inputs are finite; a program needn't handle non-finite values.
Results may differ from the reference program's by a relative error of at most 0.00036.
Values may be sent and summed in bfloat16 or wider, within the bound.
A program may use at most 192 MiB of HBM per device.

```python
import jax
import jax.numpy as jnp
from jax import lax

N = 8192
B = 4096
BS = 512
R = 128


def levels(rng, extent, cuts, smallest, high):
    def one(position, parts):
        steps = jax.random.uniform(jax.random.fold_in(jax.random.fold_in(rng, 6), position), (parts,), jnp.float32, smallest / len(cuts), high / len(cuts))
        return jnp.repeat(jnp.exp(steps), extent[position] // parts).reshape((-1,) + (1,) * (len(extent) - position - 1))

    gain = one(*cuts[0])
    for cut in cuts[1:]:
        gain = gain * one(*cut)
    return gain


def scatter_about(own_key, shape, spread, limit, shards=(), held_as=jnp.bfloat16):
    values = spread * jax.random.normal(own_key, shape, jnp.float32)
    if shards:
        values = values * levels(own_key, shape, shards, -0.22, 0.18)
    return jnp.clip(values, -limit, limit).astype(held_as)


def setup_inputs(seed: int = 0) -> dict:
    streams_of = jax.random.split(jax.random.key(seed), 7)
    trailing = scatter_about(streams_of[0], (N, N), 1.0, 6.0, ((0, 2), (1, 4)), jnp.float32)
    panel = scatter_about(streams_of[1], (N, B), 0.125, 0.75, ((0, 2), (1, 4)))
    inverse_factor = scatter_about(streams_of[2], (B, B), B ** -0.5, 0.09375, ((0, 4), (1, 4)))
    block_inverse = scatter_about(streams_of[3], (N, BS), BS ** -0.5, 0.25, ((0, 2),), jnp.float32)
    guess = scatter_about(streams_of[4], (N, R), N ** -0.5, 0.0625, ((0, 16),), jnp.float32)
    target = scatter_about(streams_of[5], (N, R), 1.0, 6.0, ((0, 2),), jnp.float32)
    return {"trailing": trailing, "panel": panel, "inverse_factor": inverse_factor, "block_inverse": block_inverse, "guess": guess, "target": target}


def reference(trailing, panel, inverse_factor, block_inverse, guess, target):
    lower = jnp.tril(inverse_factor)
    factor = jnp.dot(panel, lower.T, preferred_element_type=jnp.float32).astype(jnp.bfloat16)
    product = jnp.dot(factor, factor.T, preferred_element_type=jnp.float32)
    updated = trailing - product
    applied = jnp.dot(updated, guess, precision=lax.Precision.HIGHEST, preferred_element_type=jnp.float32)
    residual = target - applied
    residual_rms = jnp.sqrt(jnp.sum(residual * residual) / (N * R))
    blocks = jnp.tril(block_inverse.reshape(N // BS, BS, BS))
    pieces = residual.reshape(N // BS, BS, R)
    first = jnp.einsum('bij,bjr->bir', blocks, pieces, precision=lax.Precision.HIGHEST)
    second = jnp.einsum('bji,bjr->bir', blocks, first, precision=lax.Precision.HIGHEST)
    correction = second.reshape(N, R)
    return (updated, correction, residual_rms.reshape(1))
```

```python
import jax
import jax.numpy as jnp
from jax import lax
from jax.sharding import PartitionSpec as P

BS = 512
AXES = ("row", "col", "depth")
HIGHEST = lax.Precision.HIGHEST


def arrivals(n):
    table = []
    for i in range(n):
        order = []
        for step in range(1, n):
            if i + step < n:
                order.append((step, 1, i + step))
            if i - step >= 0:
                order.append((step, 0, i - step))
        table.append(order)
    return table


def choose(table, index):
    return jnp.asarray(table, jnp.int32)[index]


def line_gather(block, axis, n, index):
    table = arrivals(n)
    right, left = [block], [block]
    for step in range(1, n):
        right.append(lax.ppermute(right[-1], axis, [(i, i + 1) for i in range(step - 1, n - 1)]))
        left.append(lax.ppermute(left[-1], axis, [(i, i - 1) for i in range(1, n - step + 1)]))
    slots, origins = [], []
    for j in range(n - 1):
        kinds = sorted({table[i][j][:2] for i in range(n)})
        value = None
        for step, way in kinds:
            arrived = (left if way else right)[step]
            here = [table[i][j][:2] == (step, way) for i in range(n)]
            flag = choose([int(h) for h in here], index) > 0
            value = arrived if value is None else jnp.where(flag, arrived, value)
        slots.append(value)
        origins.append(choose([table[i][j][2] for i in range(n)], index))
    return slots, origins


def cube_gather(block, axis, n):
    found = {0: block}
    bit = n // 2
    while bit:
        for o in sorted(found):
            found[o | bit] = lax.ppermute(found[o], axis, [(i, i ^ bit) for i in range(n)])
        bit //= 2
    return [found[o] for o in range(n)]


def body(sizes, trailing, panel, inverse_factor, block_inverse, guess, target):
    n_row, n_col, n_depth = sizes
    rows_here, width_j = panel.shape
    cols_here = trailing.shape[1]
    width_k = inverse_factor.shape[0]
    row_id = lax.axis_index("row")
    col_id = lax.axis_index("col")
    depth_id = lax.axis_index("depth")
    share_rows = rows_here // n_col
    share_cols = cols_here // n_depth
    part = share_rows // n_depth
    strip = width_k // n_row

    k_index = depth_id * width_k + lax.broadcasted_iota(jnp.int32, (width_k, width_j), 0)
    j_index = col_id * width_j + lax.broadcasted_iota(jnp.int32, (width_k, width_j), 1)
    lower = jnp.where(k_index >= j_index, inverse_factor, jnp.zeros_like(inverse_factor))
    my_strip = lax.dynamic_slice_in_dim(lower, row_id * strip, strip, 0)
    strips, origins = line_gather(my_strip, "col", n_col, col_id)

    def ordered(rows):
        return jnp.concatenate(
            [lax.dynamic_slice_in_dim(rows, (depth_id ^ o) * part, part, 0) for o in range(n_depth)], 0
        )

    panels = [ordered(lax.dynamic_slice_in_dim(panel, col_id * share_rows, share_rows, 0))]
    for s in range(1, n_col):
        to = (col_id + s) % n_col
        piece = lax.dynamic_slice_in_dim(panel, to * share_rows + depth_id * part, part, 0)
        piece = lax.ppermute(piece, "col", [(i, (i + s) % n_col) for i in range(n_col)])
        panels.append(jnp.concatenate(cube_gather(piece, "depth", n_depth), 0))
    shifted = jnp.stack(panels)

    def times(rows, matrix):
        return lax.dot_general(rows, matrix, (((1,), (1,)), ((), ())), preferred_element_type=jnp.float32)

    share = times(panels[0], lower)
    for own, origin in zip(strips, origins):
        pieces = cube_gather(own, "row", n_row)
        full = jnp.zeros((width_k, width_j), lower.dtype)
        for o, piece in enumerate(pieces):
            full = lax.dynamic_update_slice_in_dim(full, piece, (row_id ^ o) * strip, 0)
        rows = lax.dynamic_index_in_dim(shifted, (col_id - origin) % n_col, 0, keepdims=False)
        share = share + times(rows, full)
    share = ordered(share.astype(jnp.bfloat16))

    mine = lax.dynamic_slice_in_dim(trailing, depth_id * share_cols, share_cols, 1)
    applied = jnp.dot(mine, guess, precision=HIGHEST, preferred_element_type=jnp.float32)
    guesses = lax.all_gather(guess, ("col", "depth"), axis=0, tiled=True)
    my_guess = lax.dynamic_slice_in_dim(guesses, row_id * rows_here + col_id * share_rows, share_rows, 0)
    wide = share.astype(jnp.float32)
    inner = lax.dot_general(
        wide, my_guess, (((0,), (0,)), ((), ())), precision=HIGHEST, preferred_element_type=jnp.float32
    )
    inner = lax.psum(inner, ("row", "col"))
    outer = jnp.dot(wide, inner, precision=HIGHEST, preferred_element_type=jnp.float32)
    at_share = lax.dynamic_slice_in_dim(applied, col_id * share_rows, share_rows, 0)
    applied = lax.dynamic_update_slice_in_dim(applied, at_share - outer, col_id * share_rows, 0)
    applied = lax.psum(applied, ("col", "depth"))
    residual = target - applied
    squares = lax.psum(jnp.sum(residual * residual), "row")
    residual_rms = jnp.sqrt(squares / (rows_here * n_row * residual.shape[1]))
    count = rows_here // BS
    blocks = jnp.tril(block_inverse.reshape(count, BS, BS))
    pieces = residual.reshape(count, BS, residual.shape[1])
    first = jnp.einsum("bij,bjr->bir", blocks, pieces, precision=HIGHEST)
    second = jnp.einsum("bji,bjr->bir", blocks, first, precision=HIGHEST)
    correction = second.reshape(rows_here, residual.shape[1])

    others, origins = line_gather(share, "col", n_col, col_id)
    held = [jnp.zeros((rows_here, width_k), share.dtype) for _ in range(n_depth)]
    for block, origin in zip([share] + others, [col_id] + origins):
        for o, piece in enumerate(cube_gather(block, "depth", n_depth)):
            held[o] = lax.dynamic_update_slice_in_dim(held[o], piece, origin * share_rows, 0)

    def owner(c, d):
        return (c * cols_here + d * share_cols) // rows_here

    def place(r, c, d):
        return (r * n_col + c) * n_depth + d

    first_row = col_id * cols_here + depth_id * share_cols
    owns = first_row // rows_here == row_id
    offset = first_row % rows_here
    updated = mine
    for o in range(n_depth):
        columns = lax.dynamic_slice_in_dim(held[o], offset, share_cols, 0)
        sent = columns
        for s in range(1, n_row):
            pairs = [
                (place(owner(c, d), c, d), place((owner(c, d) + s) % n_row, c, d))
                for c in range(n_col)
                for d in range(n_depth)
            ]
            got = lax.ppermute(sent, AXES, pairs)
            came = (first_row // rows_here + s) % n_row == row_id
            columns = jnp.where(came, got, columns)
        updated = updated - times(held[o], columns)
    return (updated, correction, residual_rms.reshape(1))


def solution(mesh):
    sizes = tuple(mesh.shape[a] for a in AXES)
    placed = (
        P("row", "col"),
        P("row", "col"),
        P("depth", "col"),
        P("row", None),
        P(("col", "depth"), None),
        P("row", None),
    )
    return jax.shard_map(
        lambda *args: body(sizes, *args),
        mesh=mesh,
        in_specs=placed,
        out_specs=(P("row", ("col", "depth")), P("row", None), P()),
        check_vma=False,
    )
```
